32 devices in a mesh: seq: 8 (over y, x, core), dp: 4 (over z).
Axes of the slice: x: 2, y: 2, z: 4, core: 2. Of those that a mesh axis runs over, the one named last changes fastest.
Arguments:
- queries: bfloat16 [4, 1024, 1536], P('dp', 'seq'), may hold values from -27 to 27
- keys: bfloat16 [4, 1024, 1536], P('dp', 'seq'), may hold values from -8 to 8
- values: bfloat16 [4, 1024, 1536], P('dp', 'seq'), may hold values from -6 to 6
- grad_out: bfloat16 [4, 1024, 1536], P('dp', 'seq'), may hold values from -6 to 6
- text_keys: bfloat16 [4, 64, 1536], P('dp', 'seq'), may hold values from -6 to 6
- text_values: bfloat16 [4, 64, 1536], P('dp', 'seq'), may hold values from -6 to 6
- null_keys: bfloat16 [64, 1536], replicated, may hold values from -6 to 6
- null_values: bfloat16 [64, 1536], replicated, may hold values from -6 to 6
- windows: int32 [64, 27], replicated, may hold values from -1 to 63, as said below
- tile_slot: int32 [64], replicated, may hold values from 0 to 63, as said below
- dropped: int32 [4], P('dp'), may hold values from 0 to 1, as said below
Outputs:
- grad_queries: bfloat16 [4, 1024, 1536], P('dp', 'seq')
- grad_keys: bfloat16 [4, 1024, 1536], P('dp', 'seq')
- grad_values: bfloat16 [4, 1024, 1536], P('dp', 'seq')
- grad_text_keys: bfloat16 [4, 64, 1536], P('dp', 'seq')
- grad_text_values: bfloat16 [4, 64, 1536], P('dp', 'seq')
- grad_null_keys: bfloat16 [64, 1536], replicated
- grad_null_values: bfloat16 [64, 1536], replicated
The draws below stay inside these ranges and needn't reach their ends.
Inputs may be any that keep to these rules, and one draw needn't show every extreme that they name: `windows`: row t lists the key tiles of query tile t = 16 g + 4 r + c: every tile of the frame pairs g - 1, g, g + 1 that exist, in the tile rows d - 1, d, d + 1 for one d with |d - r| <= 1 and 1 <= d <= 2, and in the tile columns e - 1, e, e + 1 for one e with |e - c| <= 1 and 1 <= e <= 2; each once, in any order, the other entries -1. A permutation that keeps each frame pair's tiles among that pair's slots: tile_slot[t] // 16 == t // 16; slot s holds tile-order rows 16 s to 16 s + 15. `dropped`: at least one clip with 1 and one with 0.
All inputs are finite; a program needn't handle non-finite values.
Results may differ from the reference program's by a relative error of at most 0.012.
The reference program's roundings to bfloat16 on the way count: a program that leaves them out, or rounds other values in their place, can miss the bound.
Values may be sent and summed in bfloat16 or wider, within the bound.
A program may use at most 128 MiB of HBM per device.

```python
import math
import jax
import jax.numpy as jnp
from jax import lax

H = 12
HD = 128
TXT = 64
FRAME_H = 8
FRAME_W = 16
TILE_T = 2
TILE_H = 2
TILE_W = 4
WIN = 27
TOK_DEV = 128
TOKENS = 1024
TILES = 64
TPD = 8
GW = 4
PAIR = 16
CLIPS = 4
N_SEQ = 8


def paired_fields(key):
    base = jax.random.fold_in(key, 71)
    first, second, third, fourth = jax.random.split(base, 4)
    shape = (CLIPS, TOKENS, H * HD)
    low = math.log(0.4)
    high = math.log(1.6)
    key_base = jax.random.truncated_normal(first, -5.0, 5.0, shape) * jnp.exp(jax.random.uniform(second, (CLIPS, TOKENS, 1), minval=low, maxval=high))
    query_base = jax.random.truncated_normal(third, -5.0, 5.0, shape) * jnp.exp(jax.random.uniform(fourth, (CLIPS, TOKENS, 1), minval=low, maxval=high))
    return (key_base, query_base)


def draw_queries(key, part):
    key_base, query_base = paired_fields(key)
    result = query_base
    return result.astype(jnp.bfloat16)


def draw_keys(key, part):
    key_base, query_base = paired_fields(key)
    result = key_base
    return result.astype(jnp.bfloat16)


def draw_windows(key, part):
    grid_h = FRAME_H // TILE_H
    tile_iota = jnp.arange(TILES, dtype=jnp.int32)
    pair_index = tile_iota // PAIR
    row = tile_iota % PAIR // GW
    column = tile_iota % GW
    column_jitter = jax.random.randint(jax.random.fold_in(key, 5), (TILES,), -1, 2)
    row_jitter = jax.random.randint(jax.random.fold_in(key, 7), (TILES,), -1, 2)
    centre = jnp.clip(column + column_jitter, 1, GW - 2)
    row_centre = jnp.clip(row + row_jitter, 1, grid_h - 2)
    entry = jnp.arange(WIN, dtype=jnp.int32)
    pair_step = entry // 9 - 1
    row_step = entry // 3 % 3 - 1
    column_step = entry % 3 - 1
    target_pair = pair_index[:, None] + pair_step[None, :]
    target_row = row_centre[:, None] + row_step[None, :]
    target_column = centre[:, None] + column_step[None, :]
    listed = target_pair * PAIR + target_row * GW + target_column
    listed = jnp.where((target_pair >= 0) & (target_pair < TILES // PAIR), listed, -1)
    ranks = jax.random.randint(jax.random.fold_in(key, 6), (TILES, WIN), 0, 1 << 20) * WIN + entry[None, :]
    order = jnp.argsort(ranks, axis=1)
    return jnp.take_along_axis(listed, order, axis=1).astype(jnp.int32)


def draw_tile_slot(key, part):
    tile_iota = jnp.arange(TILES, dtype=jnp.int32)
    ranks = jax.random.randint(jax.random.fold_in(key, 9), (TILES,), 0, 1 << 20) * PAIR + tile_iota % PAIR
    order = jnp.argsort(ranks.reshape(TILES // PAIR, PAIR), axis=1).astype(jnp.int32)
    return (tile_iota // PAIR * PAIR + order.reshape(TILES)).astype(jnp.int32)


def draw_dropped(key, part):
    levels = jax.random.randint(jax.random.fold_in(key, 3), (CLIPS,), 0, 4)
    flags = (levels == 0).astype(jnp.int32)
    order = jax.random.permutation(jax.random.fold_in(key, 4), CLIPS)
    flags = flags.at[order[0]].set(1)
    flags = flags.at[order[1]].set(0)
    return flags.astype(jnp.int32)


def steps_of(key, dims, shards, least, top_value):
    loudness = 1.0
    for axis_at, blocks in shards:
        steps = jax.random.uniform(jax.random.fold_in(jax.random.fold_in(key, 6), axis_at), (blocks,), jnp.float32, least / len(shards), top_value / len(shards))
        loudness = loudness * jnp.repeat(jnp.exp(steps), dims[axis_at] // blocks).reshape((-1,) + (1,) * (len(dims) - 1 - axis_at))
    return loudness


def bell_draw(rng, shape, deviation, limit, shards=(), kind=jnp.bfloat16):
    drawn = jax.random.normal(rng, shape, jnp.float32) * deviation
    if len(shards) > 0:
        drawn = steps_of(rng, shape, shards, -0.22, 0.18) * drawn
    return jnp.clip(drawn, min=-limit, max=limit).astype(kind)


def setup_inputs(seed: int = 0) -> dict:
    arg_keys = jax.random.split(jax.random.key(seed), 12)
    queries = draw_queries(jax.random.fold_in(arg_keys[11], 71), 0)
    keys = draw_keys(jax.random.fold_in(arg_keys[11], 71), 0)
    values = bell_draw(arg_keys[2], (CLIPS, TOKENS, H * HD), 1.0, 6.0, ((0, 4), (1, 8)))
    grad_out = bell_draw(arg_keys[3], (CLIPS, TOKENS, H * HD), 1.0, 6.0, ((0, 4), (1, 8)))
    text_keys = bell_draw(arg_keys[4], (CLIPS, TXT, H * HD), 1.0, 6.0, ((0, 4), (1, 8)))
    text_values = bell_draw(arg_keys[5], (CLIPS, TXT, H * HD), 1.0, 6.0, ((0, 4), (1, 8)))
    null_keys = bell_draw(arg_keys[6], (TXT, H * HD), 1.0, 6.0)
    null_values = bell_draw(arg_keys[7], (TXT, H * HD), 1.0, 6.0)
    windows = draw_windows(jax.random.fold_in(arg_keys[11], 71), 0)
    tile_slot = draw_tile_slot(jax.random.fold_in(arg_keys[11], 71), 0)
    dropped = draw_dropped(jax.random.fold_in(arg_keys[11], 71), 0)
    return dict(queries=queries, keys=keys, values=values, grad_out=grad_out, text_keys=text_keys, text_values=text_values, null_keys=null_keys, null_values=null_values, windows=windows, tile_slot=tile_slot, dropped=dropped)


def block_grads(block_queries, block_grad_out, near_keys, near_values, prompt_keys, prompt_values, allowed, score_scale):
    head_count = H
    head_queries = block_queries.reshape(-1, head_count, HD).astype(jnp.float32)
    head_grad_out = block_grad_out.reshape(-1, head_count, HD).astype(jnp.float32)
    head_keys = near_keys.reshape(-1, head_count, HD).astype(jnp.float32)
    head_values = near_values.reshape(-1, head_count, HD).astype(jnp.float32)
    text_keys_h = prompt_keys.reshape(-1, head_count, HD).astype(jnp.float32)
    text_values_h = prompt_values.reshape(-1, head_count, HD).astype(jnp.float32)
    near_scores = jnp.einsum('qhd,khd->hqk', head_queries, head_keys) * score_scale
    near_scores = jnp.where(allowed[None], near_scores, -jnp.inf)
    text_scores = jnp.einsum('qhd,khd->hqk', head_queries, text_keys_h) * score_scale
    row_top = jnp.maximum(jnp.max(near_scores, axis=-1), jnp.max(text_scores, axis=-1))
    log_total = row_top + jnp.log(jnp.sum(jnp.exp(near_scores - row_top[..., None]), axis=-1)
                                  + jnp.sum(jnp.exp(text_scores - row_top[..., None]), axis=-1))
    weights = jnp.where(allowed[None], jnp.exp(near_scores - log_total[..., None]), 0.0)
    text_weights = jnp.exp(text_scores - log_total[..., None])
    weights_low = weights.astype(jnp.bfloat16).astype(jnp.float32)
    text_low = text_weights.astype(jnp.bfloat16).astype(jnp.float32)
    attended = jnp.einsum('hqk,khd->qhd', weights_low, head_values) + jnp.einsum('hqk,khd->qhd', text_low, text_values_h)
    row_dot = jnp.transpose(jnp.sum(head_grad_out * attended, axis=-1))
    grad_weights = jnp.einsum('qhd,khd->hqk', head_grad_out, head_values)
    text_grad_weights = jnp.einsum('qhd,khd->hqk', head_grad_out, text_values_h)
    grad_scores = (weights * (grad_weights - row_dot[..., None])).astype(jnp.bfloat16).astype(jnp.float32)
    text_grad_scores = (text_weights * (text_grad_weights - row_dot[..., None])).astype(jnp.bfloat16).astype(jnp.float32)
    grad_queries = (jnp.einsum('hqk,khd->qhd', grad_scores, head_keys)
                    + jnp.einsum('hqk,khd->qhd', text_grad_scores, text_keys_h)) * score_scale
    key_part = (jnp.einsum('hqk,qhd->khd', grad_scores, head_queries) * score_scale).astype(jnp.bfloat16)
    value_part = jnp.einsum('hqk,qhd->khd', weights_low, head_grad_out).astype(jnp.bfloat16)
    prompt_k = jnp.einsum('hqk,qhd->khd', text_grad_scores, head_queries) * score_scale
    prompt_v = jnp.einsum('hqk,qhd->khd', text_low, head_grad_out)
    feature_count = head_count * HD
    parts = jnp.concatenate([key_part.reshape(-1, feature_count), value_part.reshape(-1, feature_count)], axis=1)
    prompt_part = jnp.concatenate([prompt_k.reshape(-1, feature_count), prompt_v.reshape(-1, feature_count)], axis=1)
    return grad_queries.reshape(-1, feature_count).astype(jnp.bfloat16), parts, prompt_part


def reference(queries, keys, values, grad_out, text_keys, text_values, null_keys, null_values, windows, tile_slot, dropped):
    score_scale = HD ** -0.5
    feature_count = H * HD
    grid_w = FRAME_W // TILE_W
    pair_len = (FRAME_H // TILE_H) * grid_w
    tile_len = TILE_T * TILE_H * TILE_W
    reach_devices = 3
    span_devices = 2 * reach_devices + 1
    token = jnp.arange(TOKENS, dtype=jnp.int32)
    frame = token // TOK_DEV
    inside = token % TOK_DEV
    row_pos = inside // FRAME_W
    col_pos = inside % FRAME_W
    tile_of = (frame // TILE_T) * pair_len + (row_pos // TILE_H) * grid_w + col_pos // TILE_W
    place = (frame % TILE_T) * (TILE_H * TILE_W) + (row_pos % TILE_H) * TILE_W + col_pos % TILE_W
    target = tile_slot[tile_of] * tile_len + place
    source = jnp.zeros((TOKENS,), jnp.int32).at[target].set(token)
    slot_iota = jnp.arange(TILES, dtype=jnp.int32)
    slot_tile = jnp.zeros((TILES,), jnp.int32).at[tile_slot].set(slot_iota)

    def one_clip(inputs):
        clip_q, clip_k, clip_v, clip_go, clip_tk, clip_tv, flag = inputs
        tile_q = clip_q[source]
        tile_k = clip_k[source]
        tile_v = clip_v[source]
        tile_go = clip_go[source]
        prompt_keys = jnp.where(flag == 1, null_keys, clip_tk)
        prompt_values = jnp.where(flag == 1, null_values, clip_tv)
        margin = reach_devices * TOK_DEV
        padded = jnp.pad(jnp.concatenate([tile_k, tile_v], axis=1), ((margin, margin), (0, 0)))

        def step(carry, block):
            grad_pad, prompt_acc = carry
            start = block * TOK_DEV
            block_q = lax.dynamic_slice_in_dim(tile_q, start, TOK_DEV, 0)
            block_go = lax.dynamic_slice_in_dim(tile_go, start, TOK_DEV, 0)
            near = lax.dynamic_slice_in_dim(padded, start, span_devices * TOK_DEV, 0)
            query_ids = lax.dynamic_slice_in_dim(slot_tile, block * TPD, TPD, 0)
            near_slots = (block - reach_devices) * TPD + jnp.arange(span_devices * TPD, dtype=jnp.int32)
            near_valid = (near_slots >= 0) & (near_slots < TILES)
            near_ids = jnp.where(near_valid, slot_tile[jnp.clip(near_slots, 0, TILES - 1)], -2)
            query_windows = windows[query_ids]
            tile_allowed = jnp.any(query_windows[:, :, None] == near_ids[None, None, :], axis=1)
            allowed = jnp.repeat(jnp.repeat(tile_allowed, tile_len, axis=0), tile_len, axis=1)
            grad_q, parts, prompt_part = block_grads(block_q, block_go, near[:, :feature_count], near[:, feature_count:],
                                                     prompt_keys, prompt_values, allowed, score_scale)
            current = lax.dynamic_slice_in_dim(grad_pad, start, span_devices * TOK_DEV, 0)
            grad_pad = lax.dynamic_update_slice_in_dim(grad_pad, current + parts.astype(jnp.float32), start, 0)
            return (grad_pad, prompt_acc + prompt_part), grad_q

        start_carry = (jnp.zeros((TOKENS + 2 * margin, 2 * feature_count), jnp.float32),
                       jnp.zeros((TXT, 2 * feature_count), jnp.float32))
        (grad_pad, prompt_acc), grad_blocks = lax.scan(step, start_carry, jnp.arange(N_SEQ, dtype=jnp.int32))
        grad_kv = grad_pad[margin:margin + TOKENS].astype(jnp.bfloat16)
        return grad_blocks.reshape(TOKENS, feature_count), grad_kv[:, :feature_count], grad_kv[:, feature_count:], prompt_acc

    grad_q, grad_k, grad_v, prompt_acc = lax.map(one_clip, (queries, keys, values, grad_out, text_keys, text_values, dropped))
    drop_float = dropped.astype(jnp.float32)[:, None, None]
    text_grads = (prompt_acc * (1.0 - drop_float)).astype(jnp.bfloat16)
    null_grads = jnp.sum(prompt_acc * drop_float, axis=0).astype(jnp.bfloat16)
    feature_count = H * HD
    return (grad_q, grad_k, grad_v, text_grads[:, :, :feature_count], text_grads[:, :, feature_count:],
            null_grads[:, :feature_count], null_grads[:, feature_count:])
```

```python
import functools

import jax
import jax.numpy as jnp
from jax import lax
from jax.experimental import pallas as pl
from jax.experimental.pallas import tpu as pltpu
from jax.sharding import PartitionSpec as P

HD = 128
FRAME_H = 8
FRAME_W = 16
TILE_T = 2
TILE_H = 2
TILE_W = 4


def partner(value, axis, stride):
    mask = 2**stride
    pairs = [(source, source ^ mask) for source in range(lax.axis_size(axis))]
    return lax.ppermute(value, axis, pairs)


def passed_along(x, axis, by):
    peers = lax.axis_size(axis)
    pairs = [(i, i + by) for i in range(peers) if 0 <= i + by < peers]
    return lax.ppermute(x, axis, pairs)


def tile_masked(scores, tile_allowed, tile_len, filler):
    head_count, query_rows, key_rows = scores.shape
    blocked = scores.reshape(
        head_count, query_rows // tile_len, tile_len, key_rows // tile_len, tile_len
    )
    blocked = jnp.where(tile_allowed[None, :, None, :, None], blocked, filler)
    return blocked.reshape(head_count, query_rows, key_rows)


def per_device(
    queries,
    keys,
    values,
    grad_out,
    text_keys,
    text_values,
    null_keys,
    null_values,
    windows,
    tile_slot,
    dropped,
):
    seq_count = lax.axis_size("seq")
    own_index = lax.axis_index("seq")
    local_rows = queries.shape[1]
    feature_count = queries.shape[2]
    head_size = HD
    head_count = feature_count // head_size
    score_scale = head_size ** (-0.5)
    tile_len = TILE_T * TILE_H * TILE_W
    tiles_local = local_rows // tile_len
    grid_w = FRAME_W // TILE_W
    grid_h = FRAME_H // TILE_H
    pair_len = grid_h * grid_w
    total_tiles = tiles_local * seq_count
    reach_devices = 3
    used_devices = 2 * reach_devices
    stacked = jnp.stack([queries[0], keys[0], values[0], grad_out[0]])
    halves = stacked.reshape(4, grid_h, TILE_H, grid_w, TILE_W, feature_count)
    halves = halves.transpose(0, 1, 3, 2, 4, 5).reshape(4, pair_len, TILE_H * TILE_W, feature_count)
    pair_index = own_index // 2
    parity = own_index % 2
    pair_slots = (
        lax.dynamic_slice_in_dim(tile_slot, pair_index * pair_len, pair_len) - pair_index * pair_len
    )
    slot_range = jnp.arange(pair_len, dtype=jnp.int32)
    local_tile = jnp.sum(
        jnp.where(pair_slots[None, :] == slot_range[:, None], slot_range[None, :], 0), axis=1
    )
    local_range = jnp.arange(tiles_local, dtype=jnp.int32)
    kept_halves = jnp.take(halves, local_tile[parity * tiles_local + local_range], axis=1)
    outgoing = jnp.take(halves, local_tile[(1 - parity) * tiles_local + local_range], axis=1)
    incoming = partner(outgoing, "seq", 0)
    first_half = jnp.where(parity == 0, kept_halves, incoming)
    second_half = jnp.where(parity == 0, incoming, kept_halves)
    tiled = jnp.concatenate([first_half, second_half], axis=2).reshape(4, local_rows, feature_count)
    tile_q = tiled[0]
    tile_k = tiled[1]
    tile_v = tiled[2]
    tile_go = tiled[3]
    slot_iota = jnp.arange(total_tiles, dtype=jnp.int32)
    slot_tile = jnp.sum(
        jnp.where(tile_slot[None, :] == slot_iota[:, None], slot_iota[None, :], 0), axis=1
    )
    query_ids = lax.dynamic_slice_in_dim(slot_tile, own_index * tiles_local, tiles_local)
    query_windows = jnp.take(windows, query_ids, axis=0)
    first_device = own_index - reach_devices + 1 - parity
    near_slots = first_device * tiles_local + jnp.arange(
        used_devices * tiles_local, dtype=jnp.int32
    )
    near_valid = (near_slots >= 0) & (near_slots < total_tiles)
    near_ids = jnp.where(
        near_valid, jnp.take(slot_tile, jnp.clip(near_slots, 0, total_tiles - 1)), -2
    )
    tile_allowed = jnp.any(query_windows[:, :, None] == near_ids[None, None, :], axis=1)
    pairs_kv = jnp.concatenate([tile_k, tile_v], axis=1)
    near_blocks = []
    for offset in range(-reach_devices, reach_devices + 1):
        if offset == 0:
            near_blocks.append(pairs_kv)
        else:
            near_blocks.append(passed_along(pairs_kv, "seq", -offset))
    near_all = jnp.concatenate(near_blocks, axis=0)
    near_kv = lax.dynamic_slice_in_dim(
        near_all, (1 - parity) * local_rows, used_devices * local_rows, 0
    )
    near_keys = near_kv[:, :feature_count].reshape(-1, head_count, head_size)
    near_values = near_kv[:, feature_count:].reshape(-1, head_count, head_size)
    prompt = lax.all_gather(
        jnp.concatenate([text_keys[0], text_values[0]], axis=1), "seq", axis=0, tiled=True
    )
    drop_flag = dropped[0]
    null_pair = jnp.concatenate([null_keys, null_values], axis=1)
    prompt_kv = jnp.where(drop_flag == 1, null_pair, prompt)
    prompt_keys = prompt_kv[:, :feature_count].reshape(-1, head_count, head_size)
    prompt_values = prompt_kv[:, feature_count:].reshape(-1, head_count, head_size)
    head_queries = tile_q.reshape(local_rows, head_count, head_size)
    head_grad_out = tile_go.reshape(local_rows, head_count, head_size)
    near_scores = (
        jnp.einsum("qhd,khd->hqk", head_queries, near_keys, preferred_element_type=jnp.float32)
        * score_scale
    )
    near_scores = tile_masked(near_scores, tile_allowed, tile_len, -jnp.inf)
    text_scores = (
        jnp.einsum("qhd,khd->hqk", head_queries, prompt_keys, preferred_element_type=jnp.float32)
        * score_scale
    )
    row_top = jnp.maximum(jnp.max(near_scores, axis=-1), jnp.max(text_scores, axis=-1))
    log_total = row_top + jnp.log(
        jnp.sum(jnp.exp(near_scores - row_top[..., None]), axis=-1)
        + jnp.sum(jnp.exp(text_scores - row_top[..., None]), axis=-1)
    )
    near_weights = jnp.exp(near_scores - log_total[..., None])
    text_weights = jnp.exp(text_scores - log_total[..., None])
    near_low = near_weights.astype(jnp.bfloat16)
    text_low = text_weights.astype(jnp.bfloat16)
    attended = jnp.einsum(
        "hqk,khd->qhd", near_low, near_values, preferred_element_type=jnp.float32
    ) + jnp.einsum("hqk,khd->qhd", text_low, prompt_values, preferred_element_type=jnp.float32)
    row_dot = jnp.transpose(jnp.sum(head_grad_out.astype(jnp.float32) * attended, axis=-1))
    near_grad_weights = jnp.einsum(
        "qhd,khd->hqk", head_grad_out, near_values, preferred_element_type=jnp.float32
    )
    text_grad_weights = jnp.einsum(
        "qhd,khd->hqk", head_grad_out, prompt_values, preferred_element_type=jnp.float32
    )
    near_grad_scores = (near_weights * (near_grad_weights - row_dot[..., None])).astype(
        jnp.bfloat16
    )
    text_grad_scores = (text_weights * (text_grad_weights - row_dot[..., None])).astype(
        jnp.bfloat16
    )
    grad_queries = (
        jnp.einsum("hqk,khd->qhd", near_grad_scores, near_keys, preferred_element_type=jnp.float32)
        + jnp.einsum(
            "hqk,khd->qhd", text_grad_scores, prompt_keys, preferred_element_type=jnp.float32
        )
    ) * score_scale
    grad_queries = grad_queries.reshape(local_rows, feature_count).astype(jnp.bfloat16)
    prompt_grad_k = (
        jnp.einsum(
            "hqk,qhd->khd", text_grad_scores, head_queries, preferred_element_type=jnp.float32
        )
        * score_scale
    )
    prompt_grad_v = jnp.einsum(
        "hqk,qhd->khd", text_low, head_grad_out, preferred_element_type=jnp.float32
    )
    prompt_partial = jnp.concatenate(
        [prompt_grad_k.reshape(-1, feature_count), prompt_grad_v.reshape(-1, feature_count)], axis=1
    )
    grad_total = jnp.zeros((local_rows, 2 * feature_count), jnp.float32)
    key_parts = (
        jnp.einsum(
            "hqk,qhd->khd", near_grad_scores, head_queries, preferred_element_type=jnp.float32
        )
        * score_scale
    ).astype(jnp.bfloat16)
    value_parts = jnp.einsum(
        "hqk,qhd->khd", near_low, head_grad_out, preferred_element_type=jnp.float32
    ).astype(jnp.bfloat16)
    contributions = jnp.concatenate(
        [key_parts.reshape(-1, feature_count), value_parts.reshape(-1, feature_count)], axis=1
    )
    empty_block = jnp.zeros((local_rows, 2 * feature_count), jnp.bfloat16)
    padded_parts = jnp.concatenate([empty_block, contributions, empty_block], axis=0)
    placed = lax.dynamic_slice_in_dim(
        padded_parts, parity * local_rows, (2 * reach_devices + 1) * local_rows, 0
    )
    for position, offset in enumerate(range(-reach_devices, reach_devices + 1)):
        outgoing_part = placed[position * local_rows : (position + 1) * local_rows]
        if offset == 0:
            grad_total = grad_total + outgoing_part.astype(jnp.float32)
        else:
            arrived = passed_along(outgoing_part, "seq", offset)
            grad_total = grad_total + arrived.astype(jnp.float32)
    grad_pairs = grad_total.astype(jnp.bfloat16)
    prompt_share = lax.psum_scatter(prompt_partial, "seq", scatter_dimension=0, tiled=True)
    drop_float = drop_flag.astype(jnp.float32)
    prompt_out = (prompt_share * (1.0 - drop_float)).astype(jnp.bfloat16)
    null_piece = lax.psum(prompt_share * drop_float, "dp").astype(jnp.bfloat16)
    null_out = lax.all_gather(null_piece, "seq", axis=0, tiled=True)
    return (
        grad_queries[None],
        grad_pairs[:, :feature_count][None],
        grad_pairs[:, feature_count:][None],
        prompt_out[:, :feature_count][None],
        prompt_out[:, feature_count:][None],
        null_out[:, :feature_count],
        null_out[:, feature_count:],
    )


HEADS_PER_PAIR = 3
SLOTS = 2
NT = (((1,), (1,)), ((), ()))
TN = (((0,), (0,)), ((), ()))
BLOCKED = -1e30


def dot(a, b, dims=(((1,), (0,)), ((), ()))):
    return lax.dot_general(a, b, dims, preferred_element_type=jnp.float32)


def head_kernel(
    seq_count,
    dp_count,
    q_ref,
    k_ref,
    v_ref,
    go_ref,
    tk_ref,
    tv_ref,
    nk_ref,
    nv_ref,
    windows_ref,
    slot_ref,
    drop_ref,
    dq_ref,
    dk_ref,
    dv_ref,
    dtk_ref,
    dtv_ref,
    dnk_ref,
    dnv_ref,
    inbuf,
    textbuf,
    nullbuf,
    outbuf,
    tgrad,
    zall,
    nsum,
    bias,
    perm,
    acc_k,
    acc_v,
    in_send,
    in_recv,
    text_send,
    text_recv,
    null_sem,
    out_send,
    out_recv,
    tg_send,
    tg_recv,
    z_send,
    z_recv,
    n_send,
    n_recv,
    own_null,
    r_send,
    sib_recv,
    windows_vmem,
    slot_vmem,
    drop_smem,
    small_sem,
):
    me = lax.axis_index("seq")
    clip = lax.axis_index("dp")
    chip = me // 2
    parity = me % 2
    chips = seq_count // 2
    rows = q_ref.shape[1]
    text_rows = tk_ref.shape[1]
    prompt_rows = seq_count * text_rows
    pair_rows = 2 * rows
    score_scale = HD**-0.5
    tokens = (q_ref, k_ref, v_ref, go_ref)
    texts = (tk_ref, tv_ref)
    own_slots = SLOTS - parity

    def columns(head):
        return pl.ds(pl.multiple_of(head * HD, HD), HD)

    def head_of(device, slot):
        first = HEADS_PER_PAIR * (device // 2)
        if isinstance(slot, int):
            return first + (device % 2 if slot == 0 else 2)
        return first + (1 - slot) * (device % 2) + 2 * slot

    own_row = pl.ds(pl.multiple_of(me * rows, rows), rows)

    def inward(slot, place, dest, act):
        cols = columns(head_of(dest, slot))
        for t in range(4):
            act(
                pltpu.make_async_remote_copy(
                    src_ref=tokens[t].at[0, :, cols],
                    dst_ref=inbuf.at[slot, t, own_row, :],
                    send_sem=in_send.at[slot, place, t],
                    recv_sem=in_recv.at[slot, t],
                    device_id={"seq": dest},
                    device_id_type=pl.DeviceIdType.MESH,
                )
            )
        for t in range(2):
            act(
                pltpu.make_async_remote_copy(
                    src_ref=texts[t].at[0, :, cols],
                    dst_ref=textbuf.at[slot, t, me],
                    send_sem=text_send.at[slot, place, t],
                    recv_sem=text_recv.at[slot, t],
                    device_id={"seq": dest},
                    device_id_type=pl.DeviceIdType.MESH,
                )
            )

    def inward_own(slot):
        cols = columns(head_of(me, slot))
        for t in range(4):
            pltpu.make_async_copy(
                tokens[t].at[0, :, cols], inbuf.at[slot, t, own_row, :], in_recv.at[slot, t]
            ).start()
        for t in range(2):
            pltpu.make_async_copy(
                texts[t].at[0, :, cols], textbuf.at[slot, t, me], text_recv.at[slot, t]
            ).start()
        for t, ref in enumerate((nk_ref, nv_ref)):
            pltpu.make_async_copy(ref.at[:, cols], nullbuf.at[slot, t], null_sem.at[slot, t]).start()

    def all_inward(act):
        for off in range(1, seq_count):
            inward(0, off, (me + off) % seq_count, act)
        for off in range(1, chips):
            inward(1, off, 2 * ((chip + off) % chips), act)

        @pl.when(parity == 1)
        def _():
            inward(1, 0, 2 * chip, act)

    outs = (dq_ref, dk_ref, dv_ref)
    text_outs = (dtk_ref, dtv_ref)
    null_outs = (dnk_ref, dnv_ref)

    def outward(slot, off, act, which=(0, 1, 2)):
        dest = (me + off) % seq_count
        cols = columns(head_of(me, slot))
        dest_row = pl.ds(pl.multiple_of(dest * rows, rows), rows)
        for t in which:
            act(
                pltpu.make_async_remote_copy(
                    src_ref=outbuf.at[slot, t, dest_row, :],
                    dst_ref=outs[t].at[0, :, cols],
                    send_sem=out_send.at[slot, off, t],
                    recv_sem=out_recv.at[t],
                    device_id={"seq": dest},
                    device_id_type=pl.DeviceIdType.MESH,
                )
            )
        for t in range(2) if 0 in which else ():
            act(
                pltpu.make_async_remote_copy(
                    src_ref=tgrad.at[slot, t, dest],
                    dst_ref=text_outs[t].at[0, :, cols],
                    send_sem=tg_send.at[slot, off, t],
                    recv_sem=tg_recv.at[t],
                    device_id={"seq": dest},
                    device_id_type=pl.DeviceIdType.MESH,
                )
            )

    def outward_own(slot):
        cols = columns(head_of(me, slot))
        for t in range(3):
            pltpu.make_async_copy(
                outbuf.at[slot, t, own_row, :], outs[t].at[0, :, cols], out_recv.at[t]
            ).start()
        for t in range(2):
            pltpu.make_async_copy(
                tgrad.at[slot, t, me], text_outs[t].at[0, :, cols], tg_recv.at[t]
            ).start()

    def across_clips(slot, off):
        return pltpu.make_async_remote_copy(
            src_ref=zall.at[slot, clip],
            dst_ref=zall.at[slot, clip],
            send_sem=z_send.at[slot, off],
            recv_sem=z_recv.at[slot],
            device_id={"dp": (clip + off) % dp_count},
            device_id_type=pl.DeviceIdType.MESH,
        )

    sibling = me + 1 - 2 * parity

    def null_copy(src, t, cols, send_sem, recv_sem, dest):
        return pltpu.make_async_remote_copy(
            src_ref=src,
            dst_ref=null_outs[t].at[:, cols],
            send_sem=send_sem,
            recv_sem=recv_sem,
            device_id={"seq": dest},
            device_id_type=pl.DeviceIdType.MESH,
        )

    def null_outward(slot, act):
        cols = columns(head_of(me, slot))
        for t in range(2):
            for off in range(1, chips):
                dest = 2 * ((chip + off) % chips) + parity
                sems = n_send.at[slot, off, t], n_recv.at[slot, t]
                act(null_copy(nsum.at[slot, t], t, cols, *sems, dest))
            sems = n_send.at[slot, 0, t], sib_recv.at[slot, 0, t]
            act(null_copy(nsum.at[slot, t], t, cols, *sems, sibling))

    def null_relay(slot, act):
        for t in range(2):
            for off in range(1, chips):
                source = 2 * ((chip + off) % chips) + parity
                cols = columns(head_of(source, slot))
                sems = r_send.at[slot, off, t], sib_recv.at[slot, off, t]
                act(null_copy(null_outs[t].at[:, cols], t, cols, *sems, sibling))

    def start(copy):
        copy.start()

    def sent(copy):
        copy.wait_send()

    def landed(ref, sem):
        pltpu.make_async_copy(ref, ref, sem).wait()

    small = [
        pltpu.make_async_copy(windows_ref, windows_vmem, small_sem.at[0]),
        pltpu.make_async_copy(slot_ref, slot_vmem, small_sem.at[1]),
        pltpu.make_async_copy(drop_ref, drop_smem, small_sem.at[2]),
    ]
    barrier = pltpu.get_barrier_semaphore()
    for off in range(1, seq_count):
        pl.semaphore_signal(
            barrier,
            inc=1,
            device_id={"seq": (me + off) % seq_count},
            device_id_type=pl.DeviceIdType.MESH,
        )
    for off in range(1, dp_count):
        pl.semaphore_signal(
            barrier,
            inc=1,
            device_id={"dp": (clip + off) % dp_count},
            device_id_type=pl.DeviceIdType.MESH,
        )
    for copy in small:
        copy.start()
    pl.semaphore_wait(barrier, seq_count - 1 + dp_count - 1)
    all_inward(start)
    inward_own(0)

    @pl.when(parity == 0)
    def _():
        inward_own(1)

    for copy in small:
        copy.wait()

    total_rows = seq_count * rows
    tile_count = windows_ref.shape[1]
    grid_w = FRAME_W // TILE_W
    pair_tiles = tile_count // chips
    tile_len = TILE_T * TILE_H * TILE_W

    def tile_of(token):
        inside = token % rows
        return (
            pair_tiles * (token // pair_rows)
            + grid_w * (inside // FRAME_W // TILE_H)
            + inside % FRAME_W // TILE_W
        )

    token = lax.broadcasted_iota(jnp.int32, (total_rows, tile_count), 0)
    tile = lax.broadcasted_iota(jnp.int32, (total_rows, tile_count), 1)
    member = jnp.where(tile_of(token) == tile, 1.0, 0.0).astype(jnp.bfloat16)
    listed = jnp.zeros((tile_count, tile_count), jnp.float32)
    key_tile = lax.broadcasted_iota(jnp.int32, (tile_count, tile_count), 0)
    for entry in range(windows_ref.shape[0]):
        listed = jnp.where(windows_vmem[entry : entry + 1, :] == key_tile, 1.0, listed)
    by_key = dot(member, listed.astype(jnp.bfloat16)).astype(jnp.bfloat16)
    spans = []
    for pair in range(chips):
        low, high = max(pair - 1, 0) * pair_rows, min(pair + 2, chips) * pair_rows
        spans.append((low, high))
        own = slice(pair * pair_rows, (pair + 1) * pair_rows)
        allowed = dot(by_key[low:high], member[own], NT)
        bias[pair, : high - low, :] = (1.0 - allowed) * BLOCKED
        slots = jnp.broadcast_to(slot_vmem[...].astype(jnp.float32), (8, tile_count))
        slot_row = dot(slots.astype(jnp.bfloat16), member[own], NT)[0:1]
        n = lax.broadcasted_iota(jnp.int32, (1, pair_rows), 1)
        inside = n % rows
        place = (
            (n // rows) * (TILE_H * TILE_W)
            + (inside // FRAME_W % TILE_H) * TILE_W
            + inside % TILE_W
        )
        target = (slot_row.astype(jnp.int32) - pair * pair_tiles) * tile_len + place
        row = lax.broadcasted_iota(jnp.int32, (pair_rows, pair_rows), 0)
        perm[pair] = jnp.where(row == target, 1.0, 0.0).astype(jnp.bfloat16)

    is_dropped = drop_smem[0] == 1

    def null_sum(slot):
        landed(zall.at[slot, pl.ds(0, dp_count - 1)], z_recv.at[slot])
        total = zall[slot, 0]
        for peer in range(1, dp_count):
            total = total + zall[slot, peer]
        for t in range(2):
            nsum[slot, t] = total[t * prompt_rows : (t + 1) * prompt_rows].astype(jnp.bfloat16)
        cols = columns(head_of(me, slot))
        null_outward(slot, start)
        for t in range(2):
            pltpu.make_async_copy(
                nsum.at[slot, t], null_outs[t].at[:, cols], own_null.at[slot, t]
            ).start()

    def one_head(slot, carry):
        for t in range(4):
            landed(inbuf.at[slot, t], in_recv.at[slot, t])
        for t in range(2):
            landed(textbuf.at[slot, t], text_recv.at[slot, t])
            landed(nullbuf.at[slot, t], null_sem.at[slot, t])
        prompt = []
        for t in range(2):
            text = textbuf[slot, t].astype(jnp.float32).reshape(prompt_rows, HD)
            null = nullbuf[slot, t].astype(jnp.float32)
            prompt.append(jnp.where(is_dropped, null, text).astype(jnp.bfloat16))
        prompt_k, prompt_v = prompt
        prompt_dk = jnp.zeros((prompt_rows, HD), jnp.float32)
        prompt_dv = jnp.zeros((prompt_rows, HD), jnp.float32)
        acc_k[...] = jnp.zeros_like(acc_k)
        acc_v[...] = jnp.zeros_like(acc_v)
        for pair in range(chips):
            low, high = spans[pair]
            own = slice(pair * pair_rows, (pair + 1) * pair_rows)
            q = inbuf[slot, 0, own, :]
            go = inbuf[slot, 3, own, :]
            near_k = inbuf[slot, 1, low:high, :]
            near_v = inbuf[slot, 2, low:high, :]
            near = dot(near_k, q, NT) * score_scale + bias[pair, : high - low, :]
            text = dot(prompt_k, q, NT) * score_scale
            top = jnp.maximum(
                jnp.max(near, axis=0, keepdims=True), jnp.max(text, axis=0, keepdims=True)
            )
            near = jnp.exp(near - top)
            text = jnp.exp(text - top)
            share = 1.0 / (
                jnp.sum(near, axis=0, keepdims=True) + jnp.sum(text, axis=0, keepdims=True)
            )
            near = near * share
            text = text * share
            near_low = near.astype(jnp.bfloat16)
            text_low = text.astype(jnp.bfloat16)
            near_g = dot(near_v, go, NT)
            text_g = dot(prompt_v, go, NT)
            row_dot = jnp.sum(
                near_low.astype(jnp.float32) * near_g, axis=0, keepdims=True
            ) + jnp.sum(text_low.astype(jnp.float32) * text_g, axis=0, keepdims=True)
            near_ds = (near * (near_g - row_dot)).astype(jnp.bfloat16)
            text_ds = (text * (text_g - row_dot)).astype(jnp.bfloat16)
            dq = (dot(near_ds, near_k, TN) + dot(text_ds, prompt_k, TN)) * score_scale
            outbuf[slot, 0, own, :] = dot(perm[pair], dq.astype(jnp.bfloat16)).astype(jnp.bfloat16)
            acc_k[low:high, :] += dot(near_ds, q)
            acc_v[low:high, :] += dot(near_low, go)
            prompt_dk += dot(text_ds, q)
            prompt_dv += dot(text_low, go)
        prompt_dk = prompt_dk * score_scale
        drop_scale = jnp.where(is_dropped, 1.0, 0.0)
        keep_scale = 1.0 - drop_scale
        for t, grad in enumerate((prompt_dk, prompt_dv)):
            kept = (grad * keep_scale).reshape(seq_count, text_rows, HD)
            tgrad[slot, t] = kept.astype(jnp.bfloat16)
            zall[slot, clip, t * prompt_rows : (t + 1) * prompt_rows, :] = grad * drop_scale
        for off in range(1, dp_count):
            across_clips(slot, off).start()

        @pl.when(slot == 1)
        def _():
            null_sum(0)

        for off in range(1, seq_count):
            outward(slot, off, start, (0,))
        for pair in range(chips):
            own = slice(pair * pair_rows, (pair + 1) * pair_rows)
            dk = (acc_k[own, :] * score_scale).astype(jnp.bfloat16)
            outbuf[slot, 1, own, :] = dot(perm[pair], dk).astype(jnp.bfloat16)
            dv = acc_v[own, :].astype(jnp.bfloat16)
            outbuf[slot, 2, own, :] = dot(perm[pair], dv).astype(jnp.bfloat16)
        for off in range(1, seq_count):
            outward(slot, off, start, (1, 2))
        outward_own(slot)
        return carry

    lax.fori_loop(0, own_slots, one_head, 0)
    null_sum(own_slots - 1)

    def pass_on(slot, carry):
        for t in range(2):
            landed(null_outs[t].at[:, 0 : (chips - 1) * HD], n_recv.at[slot, t])
        null_relay(slot, start)
        return carry

    lax.fori_loop(0, own_slots, pass_on, 0)

    all_inward(sent)

    def drain(slot, carry):
        for off in range(1, dp_count):
            across_clips(slot, off).wait_send()
        for off in range(1, seq_count):
            outward(slot, off, sent)
        null_outward(slot, sent)
        null_relay(slot, sent)
        for t in range(2):
            landed(nsum.at[slot, t], own_null.at[slot, t])
        return carry

    def from_sibling(slot, carry):
        for t in range(2):
            for place in range(chips):
                landed(null_outs[t].at[:, 0:HD], sib_recv.at[slot, place, t])
        return carry

    lax.fori_loop(0, own_slots, drain, 0)
    for t in range(3):
        landed(outs[t], out_recv.at[t])
    for t in range(2):
        landed(text_outs[t], tg_recv.at[t])
    lax.fori_loop(0, 1 + parity, from_sibling, 0)


def hand_over(*refs):
    count = (len(refs) - 1) // 2
    sources, results, out_of = refs[:count], refs[count : 2 * count], refs[2 * count]
    stores = [pltpu.make_async_copy(sources[i], results[i], out_of.at[i]) for i in range(count)]
    for store in stores:
        store.start()
    for store in stores:
        store.wait()


def by_heads(
    dp_count,
    queries,
    keys,
    values,
    grad_out,
    text_keys,
    text_values,
    null_keys,
    null_values,
    windows,
    tile_slot,
    dropped,
):
    seq_count = lax.axis_size("seq")
    rows = queries.shape[1]
    total_rows = seq_count * rows
    pair_rows = 2 * rows
    text_rows = text_keys.shape[1]
    prompt_rows = text_rows * seq_count
    chips = seq_count // 2
    bf16, f32 = jnp.bfloat16, jnp.float32
    dma = pltpu.SemaphoreType.DMA
    hbm = pl.BlockSpec(memory_space=pl.ANY)
    like = [queries, keys, values, text_keys, text_values, null_keys, null_values]
    gathered = pl.pallas_call(
        functools.partial(head_kernel, seq_count, dp_count),
        out_shape=tuple(jax.ShapeDtypeStruct(x.shape, x.dtype) for x in like),
        in_specs=[hbm] * 11,
        out_specs=tuple([hbm] * 7),
        scratch_shapes=[
            pltpu.VMEM((SLOTS, 4, total_rows, HD), bf16),
            pltpu.VMEM((SLOTS, 2, seq_count, text_rows, HD), bf16),
            pltpu.VMEM((SLOTS, 2, prompt_rows, HD), bf16),
            pltpu.VMEM((SLOTS, 3, total_rows, HD), bf16),
            pltpu.VMEM((SLOTS, 2, seq_count, text_rows, HD), bf16),
            pltpu.VMEM((SLOTS, dp_count, 2 * prompt_rows, HD), f32),
            pltpu.VMEM((SLOTS, 2, prompt_rows, HD), bf16),
            pltpu.VMEM((chips, 3 * pair_rows, pair_rows), f32),
            pltpu.VMEM((chips, pair_rows, pair_rows), bf16),
            pltpu.VMEM((total_rows, HD), f32),
            pltpu.VMEM((total_rows, HD), f32),
            dma((SLOTS, seq_count, 4)),
            dma((SLOTS, 4)),
            dma((SLOTS, seq_count, 2)),
            dma((SLOTS, 2)),
            dma((SLOTS, 2)),
            dma((SLOTS, seq_count, 3)),
            dma((3,)),
            dma((SLOTS, seq_count, 2)),
            dma((2,)),
            dma((SLOTS, dp_count)),
            dma((SLOTS,)),
            dma((SLOTS, chips, 2)),
            dma((SLOTS, 2)),
            dma((SLOTS, 2)),
            dma((SLOTS, chips, 2)),
            dma((SLOTS, chips, 2)),
            pltpu.VMEM(windows.shape[::-1], jnp.int32),
            pltpu.VMEM((1, tile_slot.shape[0]), jnp.int32),
            pltpu.SMEM(dropped.shape, jnp.int32),
            dma((3,)),
        ],
        compiler_params=pltpu.CompilerParams(
            collective_id=0, has_side_effects=True, vmem_limit_bytes=24 * 2**20
        ),
    )(
        *(
            pltpu.with_memory_space_constraint(x, pltpu.HBM)
            for x in (
                queries,
                keys,
                values,
                grad_out,
                text_keys,
                text_values,
                null_keys,
                null_values,
                windows.T,
                tile_slot.reshape(1, -1),
            )
        ),
        dropped,
    )
    return pl.pallas_call(
        hand_over,
        out_shape=tuple(jax.ShapeDtypeStruct(x.shape, x.dtype) for x in like),
        in_specs=[hbm] * 7,
        out_specs=tuple([hbm] * 7),
        scratch_shapes=[dma((7,))],
        compiler_params=pltpu.CompilerParams(vmem_limit_bytes=2 * 2**20),
    )(*gathered)


def device_program(mesh):
    seq_count, dp_count = mesh.shape["seq"], mesh.shape["dp"]

    def program(*arrays):
        head_count = arrays[0].shape[2] // HD
        if seq_count % 2 == 0 and 2 * head_count == HEADS_PER_PAIR * seq_count:
            return by_heads(dp_count, *arrays)
        return per_device(*arrays)

    return program


def solution(mesh):
    in_specs = (
        P("dp", "seq", None),
        P("dp", "seq", None),
        P("dp", "seq", None),
        P("dp", "seq", None),
        P("dp", "seq", None),
        P("dp", "seq", None),
        P(),
        P(),
        P(),
        P(),
        P("dp"),
    )
    out_specs = (
        P("dp", "seq", None),
        P("dp", "seq", None),
        P("dp", "seq", None),
        P("dp", "seq", None),
        P("dp", "seq", None),
        P(),
        P(),
    )
    return jax.shard_map(
        device_program(mesh), mesh=mesh, in_specs=in_specs, out_specs=out_specs, check_vma=False
    )
```

```python
import functools

import jax
import jax.numpy as jnp
from jax import lax
from jax.experimental import pallas as pl
from jax.experimental.pallas import tpu as pltpu
from jax.sharding import PartitionSpec as P

HD = 128
FRAME_H = 8
FRAME_W = 16
TILE_T = 2
TILE_H = 2
TILE_W = 4


def partner(value, axis, stride):
    mask = 2**stride
    pairs = [(source, source ^ mask) for source in range(lax.axis_size(axis))]
    return lax.ppermute(value, axis, pairs)


def passed_along(x, axis, by):
    peers = lax.axis_size(axis)
    pairs = [(i, i + by) for i in range(peers) if 0 <= i + by < peers]
    return lax.ppermute(x, axis, pairs)


def tile_masked(scores, tile_allowed, tile_len, filler):
    head_count, query_rows, key_rows = scores.shape
    blocked = scores.reshape(
        head_count, query_rows // tile_len, tile_len, key_rows // tile_len, tile_len
    )
    blocked = jnp.where(tile_allowed[None, :, None, :, None], blocked, filler)
    return blocked.reshape(head_count, query_rows, key_rows)


def per_device(
    queries,
    keys,
    values,
    grad_out,
    text_keys,
    text_values,
    null_keys,
    null_values,
    windows,
    tile_slot,
    dropped,
):
    seq_count = lax.axis_size("seq")
    own_index = lax.axis_index("seq")
    local_rows = queries.shape[1]
    feature_count = queries.shape[2]
    head_size = HD
    head_count = feature_count // head_size
    score_scale = head_size ** (-0.5)
    tile_len = TILE_T * TILE_H * TILE_W
    tiles_local = local_rows // tile_len
    grid_w = FRAME_W // TILE_W
    grid_h = FRAME_H // TILE_H
    pair_len = grid_h * grid_w
    total_tiles = tiles_local * seq_count
    reach_devices = 3
    used_devices = 2 * reach_devices
    stacked = jnp.stack([queries[0], keys[0], values[0], grad_out[0]])
    halves = stacked.reshape(4, grid_h, TILE_H, grid_w, TILE_W, feature_count)
    halves = halves.transpose(0, 1, 3, 2, 4, 5).reshape(4, pair_len, TILE_H * TILE_W, feature_count)
    pair_index = own_index // 2
    parity = own_index % 2
    pair_slots = (
        lax.dynamic_slice_in_dim(tile_slot, pair_index * pair_len, pair_len) - pair_index * pair_len
    )
    slot_range = jnp.arange(pair_len, dtype=jnp.int32)
    local_tile = jnp.sum(
        jnp.where(pair_slots[None, :] == slot_range[:, None], slot_range[None, :], 0), axis=1
    )
    local_range = jnp.arange(tiles_local, dtype=jnp.int32)
    kept_halves = jnp.take(halves, local_tile[parity * tiles_local + local_range], axis=1)
    outgoing = jnp.take(halves, local_tile[(1 - parity) * tiles_local + local_range], axis=1)
    incoming = partner(outgoing, "seq", 0)
    first_half = jnp.where(parity == 0, kept_halves, incoming)
    second_half = jnp.where(parity == 0, incoming, kept_halves)
    tiled = jnp.concatenate([first_half, second_half], axis=2).reshape(4, local_rows, feature_count)
    tile_q = tiled[0]
    tile_k = tiled[1]
    tile_v = tiled[2]
    tile_go = tiled[3]
    slot_iota = jnp.arange(total_tiles, dtype=jnp.int32)
    slot_tile = jnp.sum(
        jnp.where(tile_slot[None, :] == slot_iota[:, None], slot_iota[None, :], 0), axis=1
    )
    query_ids = lax.dynamic_slice_in_dim(slot_tile, own_index * tiles_local, tiles_local)
    query_windows = jnp.take(windows, query_ids, axis=0)
    first_device = own_index - reach_devices + 1 - parity
    near_slots = first_device * tiles_local + jnp.arange(
        used_devices * tiles_local, dtype=jnp.int32
    )
    near_valid = (near_slots >= 0) & (near_slots < total_tiles)
    near_ids = jnp.where(
        near_valid, jnp.take(slot_tile, jnp.clip(near_slots, 0, total_tiles - 1)), -2
    )
    tile_allowed = jnp.any(query_windows[:, :, None] == near_ids[None, None, :], axis=1)
    pairs_kv = jnp.concatenate([tile_k, tile_v], axis=1)
    near_blocks = []
    for offset in range(-reach_devices, reach_devices + 1):
        if offset == 0:
            near_blocks.append(pairs_kv)
        else:
            near_blocks.append(passed_along(pairs_kv, "seq", -offset))
    near_all = jnp.concatenate(near_blocks, axis=0)
    near_kv = lax.dynamic_slice_in_dim(
        near_all, (1 - parity) * local_rows, used_devices * local_rows, 0
    )
    near_keys = near_kv[:, :feature_count].reshape(-1, head_count, head_size)
    near_values = near_kv[:, feature_count:].reshape(-1, head_count, head_size)
    prompt = lax.all_gather(
        jnp.concatenate([text_keys[0], text_values[0]], axis=1), "seq", axis=0, tiled=True
    )
    drop_flag = dropped[0]
    null_pair = jnp.concatenate([null_keys, null_values], axis=1)
    prompt_kv = jnp.where(drop_flag == 1, null_pair, prompt)
    prompt_keys = prompt_kv[:, :feature_count].reshape(-1, head_count, head_size)
    prompt_values = prompt_kv[:, feature_count:].reshape(-1, head_count, head_size)
    head_queries = tile_q.reshape(local_rows, head_count, head_size)
    head_grad_out = tile_go.reshape(local_rows, head_count, head_size)
    near_scores = (
        jnp.einsum("qhd,khd->hqk", head_queries, near_keys, preferred_element_type=jnp.float32)
        * score_scale
    )
    near_scores = tile_masked(near_scores, tile_allowed, tile_len, -jnp.inf)
    text_scores = (
        jnp.einsum("qhd,khd->hqk", head_queries, prompt_keys, preferred_element_type=jnp.float32)
        * score_scale
    )
    row_top = jnp.maximum(jnp.max(near_scores, axis=-1), jnp.max(text_scores, axis=-1))
    log_total = row_top + jnp.log(
        jnp.sum(jnp.exp(near_scores - row_top[..., None]), axis=-1)
        + jnp.sum(jnp.exp(text_scores - row_top[..., None]), axis=-1)
    )
    near_weights = jnp.exp(near_scores - log_total[..., None])
    text_weights = jnp.exp(text_scores - log_total[..., None])
    near_low = near_weights.astype(jnp.bfloat16)
    text_low = text_weights.astype(jnp.bfloat16)
    attended = jnp.einsum(
        "hqk,khd->qhd", near_low, near_values, preferred_element_type=jnp.float32
    ) + jnp.einsum("hqk,khd->qhd", text_low, prompt_values, preferred_element_type=jnp.float32)
    row_dot = jnp.transpose(jnp.sum(head_grad_out.astype(jnp.float32) * attended, axis=-1))
    near_grad_weights = jnp.einsum(
        "qhd,khd->hqk", head_grad_out, near_values, preferred_element_type=jnp.float32
    )
    text_grad_weights = jnp.einsum(
        "qhd,khd->hqk", head_grad_out, prompt_values, preferred_element_type=jnp.float32
    )
    near_grad_scores = (near_weights * (near_grad_weights - row_dot[..., None])).astype(
        jnp.bfloat16
    )
    text_grad_scores = (text_weights * (text_grad_weights - row_dot[..., None])).astype(
        jnp.bfloat16
    )
    grad_queries = (
        jnp.einsum("hqk,khd->qhd", near_grad_scores, near_keys, preferred_element_type=jnp.float32)
        + jnp.einsum(
            "hqk,khd->qhd", text_grad_scores, prompt_keys, preferred_element_type=jnp.float32
        )
    ) * score_scale
    grad_queries = grad_queries.reshape(local_rows, feature_count).astype(jnp.bfloat16)
    prompt_grad_k = (
        jnp.einsum(
            "hqk,qhd->khd", text_grad_scores, head_queries, preferred_element_type=jnp.float32
        )
        * score_scale
    )
    prompt_grad_v = jnp.einsum(
        "hqk,qhd->khd", text_low, head_grad_out, preferred_element_type=jnp.float32
    )
    prompt_partial = jnp.concatenate(
        [prompt_grad_k.reshape(-1, feature_count), prompt_grad_v.reshape(-1, feature_count)], axis=1
    )
    grad_total = jnp.zeros((local_rows, 2 * feature_count), jnp.float32)
    key_parts = (
        jnp.einsum(
            "hqk,qhd->khd", near_grad_scores, head_queries, preferred_element_type=jnp.float32
        )
        * score_scale
    ).astype(jnp.bfloat16)
    value_parts = jnp.einsum(
        "hqk,qhd->khd", near_low, head_grad_out, preferred_element_type=jnp.float32
    ).astype(jnp.bfloat16)
    contributions = jnp.concatenate(
        [key_parts.reshape(-1, feature_count), value_parts.reshape(-1, feature_count)], axis=1
    )
    empty_block = jnp.zeros((local_rows, 2 * feature_count), jnp.bfloat16)
    padded_parts = jnp.concatenate([empty_block, contributions, empty_block], axis=0)
    placed = lax.dynamic_slice_in_dim(
        padded_parts, parity * local_rows, (2 * reach_devices + 1) * local_rows, 0
    )
    for position, offset in enumerate(range(-reach_devices, reach_devices + 1)):
        outgoing_part = placed[position * local_rows : (position + 1) * local_rows]
        if offset == 0:
            grad_total = grad_total + outgoing_part.astype(jnp.float32)
        else:
            arrived = passed_along(outgoing_part, "seq", offset)
            grad_total = grad_total + arrived.astype(jnp.float32)
    grad_pairs = grad_total.astype(jnp.bfloat16)
    prompt_share = lax.psum_scatter(prompt_partial, "seq", scatter_dimension=0, tiled=True)
    drop_float = drop_flag.astype(jnp.float32)
    prompt_out = (prompt_share * (1.0 - drop_float)).astype(jnp.bfloat16)
    null_piece = lax.psum(prompt_share * drop_float, "dp").astype(jnp.bfloat16)
    null_out = lax.all_gather(null_piece, "seq", axis=0, tiled=True)
    return (
        grad_queries[None],
        grad_pairs[:, :feature_count][None],
        grad_pairs[:, feature_count:][None],
        prompt_out[:, :feature_count][None],
        prompt_out[:, feature_count:][None],
        null_out[:, :feature_count],
        null_out[:, feature_count:],
    )


HEADS_PER_PAIR = 3
SLOTS = 2
NT = (((1,), (1,)), ((), ()))
TN = (((0,), (0,)), ((), ()))
BLOCKED = -1e30


def dot(a, b, dims=(((1,), (0,)), ((), ()))):
    return lax.dot_general(a, b, dims, preferred_element_type=jnp.float32)


def head_kernel(
    seq_count,
    dp_count,
    q_ref,
    k_ref,
    v_ref,
    go_ref,
    tk_ref,
    tv_ref,
    nk_ref,
    nv_ref,
    windows_ref,
    slot_ref,
    drop_ref,
    dq_ref,
    dk_ref,
    dv_ref,
    dtk_ref,
    dtv_ref,
    dnk_ref,
    dnv_ref,
    inbuf,
    textbuf,
    nullbuf,
    outbuf,
    tgrad,
    zall,
    nsum,
    bias,
    perm,
    acc_k,
    acc_v,
    in_send,
    in_recv,
    text_send,
    text_recv,
    null_sem,
    out_send,
    out_recv,
    tg_send,
    tg_recv,
    z_send,
    z_recv,
    n_send,
    n_recv,
    own_null,
    r_send,
    sib_recv,
    windows_vmem,
    slot_vmem,
    drop_smem,
    small_sem,
):
    me = lax.axis_index("seq")
    clip = lax.axis_index("dp")
    chip = me // 2
    parity = me % 2
    chips = seq_count // 2
    rows = q_ref.shape[1]
    text_rows = tk_ref.shape[1]
    prompt_rows = seq_count * text_rows
    pair_rows = 2 * rows
    score_scale = HD**-0.5
    tokens = (q_ref, k_ref, v_ref, go_ref)
    texts = (tk_ref, tv_ref)
    own_slots = SLOTS - parity

    def columns(head):
        return pl.ds(pl.multiple_of(head * HD, HD), HD)

    def head_of(device, slot):
        first = HEADS_PER_PAIR * (device // 2)
        if isinstance(slot, int):
            return first + (device % 2 if slot == 0 else 2)
        return first + (1 - slot) * (device % 2) + 2 * slot

    own_row = pl.ds(pl.multiple_of(me * rows, rows), rows)

    def inward(slot, place, dest, act):
        cols = columns(head_of(dest, slot))
        for t in range(4):
            act(
                pltpu.make_async_remote_copy(
                    src_ref=tokens[t].at[0, :, cols],
                    dst_ref=inbuf.at[slot, t, own_row, :],
                    send_sem=in_send.at[slot, place, t],
                    recv_sem=in_recv.at[slot, t],
                    device_id={"seq": dest},
                    device_id_type=pl.DeviceIdType.MESH,
                )
            )
        for t in range(2):
            act(
                pltpu.make_async_remote_copy(
                    src_ref=texts[t].at[0, :, cols],
                    dst_ref=textbuf.at[slot, t, me],
                    send_sem=text_send.at[slot, place, t],
                    recv_sem=text_recv.at[slot, t],
                    device_id={"seq": dest},
                    device_id_type=pl.DeviceIdType.MESH,
                )
            )

    def inward_own(slot):
        cols = columns(head_of(me, slot))
        for t in range(4):
            pltpu.make_async_copy(
                tokens[t].at[0, :, cols], inbuf.at[slot, t, own_row, :], in_recv.at[slot, t]
            ).start()
        for t in range(2):
            pltpu.make_async_copy(
                texts[t].at[0, :, cols], textbuf.at[slot, t, me], text_recv.at[slot, t]
            ).start()
        for t, ref in enumerate((nk_ref, nv_ref)):
            pltpu.make_async_copy(ref.at[:, cols], nullbuf.at[slot, t], null_sem.at[slot, t]).start()

    def all_inward(act):
        for off in range(1, seq_count):
            inward(0, off, (me + off) % seq_count, act)
        for off in range(1, chips):
            inward(1, off, 2 * ((chip + off) % chips), act)

        @pl.when(parity == 1)
        def _():
            inward(1, 0, 2 * chip, act)

    outs = (dq_ref, dk_ref, dv_ref)
    text_outs = (dtk_ref, dtv_ref)
    null_outs = (dnk_ref, dnv_ref)

    def outward(slot, off, act, which=(0, 1, 2)):
        dest = (me + off) % seq_count
        cols = columns(head_of(me, slot))
        dest_row = pl.ds(pl.multiple_of(dest * rows, rows), rows)
        for t in which:
            act(
                pltpu.make_async_remote_copy(
                    src_ref=outbuf.at[slot, t, dest_row, :],
                    dst_ref=outs[t].at[0, :, cols],
                    send_sem=out_send.at[slot, off, t],
                    recv_sem=out_recv.at[t],
                    device_id={"seq": dest},
                    device_id_type=pl.DeviceIdType.MESH,
                )
            )
        for t in range(2) if 0 in which else ():
            act(
                pltpu.make_async_remote_copy(
                    src_ref=tgrad.at[slot, t, dest],
                    dst_ref=text_outs[t].at[0, :, cols],
                    send_sem=tg_send.at[slot, off, t],
                    recv_sem=tg_recv.at[t],
                    device_id={"seq": dest},
                    device_id_type=pl.DeviceIdType.MESH,
                )
            )

    def outward_own(slot):
        cols = columns(head_of(me, slot))
        for t in range(3):
            pltpu.make_async_copy(
                outbuf.at[slot, t, own_row, :], outs[t].at[0, :, cols], out_recv.at[t]
            ).start()
        for t in range(2):
            pltpu.make_async_copy(
                tgrad.at[slot, t, me], text_outs[t].at[0, :, cols], tg_recv.at[t]
            ).start()

    def across_clips(slot, off):
        return pltpu.make_async_remote_copy(
            src_ref=zall.at[slot, clip],
            dst_ref=zall.at[slot, clip],
            send_sem=z_send.at[slot, off],
            recv_sem=z_recv.at[slot],
            device_id={"dp": (clip + off) % dp_count},
            device_id_type=pl.DeviceIdType.MESH,
        )

    sibling = me + 1 - 2 * parity

    def null_copy(src, t, cols, send_sem, recv_sem, dest):
        return pltpu.make_async_remote_copy(
            src_ref=src,
            dst_ref=null_outs[t].at[:, cols],
            send_sem=send_sem,
            recv_sem=recv_sem,
            device_id={"seq": dest},
            device_id_type=pl.DeviceIdType.MESH,
        )

    def null_outward(slot, act):
        cols = columns(head_of(me, slot))
        for t in range(2):
            for off in range(1, chips):
                dest = 2 * ((chip + off) % chips) + parity
                sems = n_send.at[slot, off, t], n_recv.at[slot, t]
                act(null_copy(nsum.at[slot, t], t, cols, *sems, dest))
            sems = n_send.at[slot, 0, t], sib_recv.at[slot, 0, t]
            act(null_copy(nsum.at[slot, t], t, cols, *sems, sibling))

    def null_relay(slot, act):
        for t in range(2):
            for off in range(1, chips):
                source = 2 * ((chip + off) % chips) + parity
                cols = columns(head_of(source, slot))
                sems = r_send.at[slot, off, t], sib_recv.at[slot, off, t]
                act(null_copy(null_outs[t].at[:, cols], t, cols, *sems, sibling))

    def start(copy):
        copy.start()

    def sent(copy):
        copy.wait_send()

    def landed(ref, sem):
        pltpu.make_async_copy(ref, ref, sem).wait()

    small = [
        pltpu.make_async_copy(windows_ref, windows_vmem, small_sem.at[0]),
        pltpu.make_async_copy(slot_ref, slot_vmem, small_sem.at[1]),
        pltpu.make_async_copy(drop_ref, drop_smem, small_sem.at[2]),
    ]
    barrier = pltpu.get_barrier_semaphore()
    for off in range(1, seq_count):
        pl.semaphore_signal(
            barrier,
            inc=1,
            device_id={"seq": (me + off) % seq_count},
            device_id_type=pl.DeviceIdType.MESH,
        )
    for off in range(1, dp_count):
        pl.semaphore_signal(
            barrier,
            inc=1,
            device_id={"dp": (clip + off) % dp_count},
            device_id_type=pl.DeviceIdType.MESH,
        )
    for copy in small:
        copy.start()
    pl.semaphore_wait(barrier, seq_count - 1 + dp_count - 1)
    all_inward(start)
    inward_own(0)

    @pl.when(parity == 0)
    def _():
        inward_own(1)

    for copy in small:
        copy.wait()

    total_rows = seq_count * rows
    tile_count = windows_ref.shape[1]
    grid_w = FRAME_W // TILE_W
    pair_tiles = tile_count // chips
    tile_len = TILE_T * TILE_H * TILE_W

    def tile_of(token):
        inside = token % rows
        return (
            pair_tiles * (token // pair_rows)
            + grid_w * (inside // FRAME_W // TILE_H)
            + inside % FRAME_W // TILE_W
        )

    token = lax.broadcasted_iota(jnp.int32, (total_rows, tile_count), 0)
    tile = lax.broadcasted_iota(jnp.int32, (total_rows, tile_count), 1)
    member = jnp.where(tile_of(token) == tile, 1.0, 0.0).astype(jnp.bfloat16)
    listed = jnp.zeros((tile_count, tile_count), jnp.float32)
    key_tile = lax.broadcasted_iota(jnp.int32, (tile_count, tile_count), 0)
    for entry in range(windows_ref.shape[0]):
        listed = jnp.where(windows_vmem[entry : entry + 1, :] == key_tile, 1.0, listed)
    by_key = dot(member, listed.astype(jnp.bfloat16)).astype(jnp.bfloat16)
    spans = []
    for pair in range(chips):
        low, high = max(pair - 1, 0) * pair_rows, min(pair + 2, chips) * pair_rows
        spans.append((low, high))
        own = slice(pair * pair_rows, (pair + 1) * pair_rows)
        allowed = dot(by_key[low:high], member[own], NT)
        bias[pair, : high - low, :] = (1.0 - allowed) * BLOCKED
        slots = jnp.broadcast_to(slot_vmem[...].astype(jnp.float32), (8, tile_count))
        slot_row = dot(slots.astype(jnp.bfloat16), member[own], NT)[0:1]
        n = lax.broadcasted_iota(jnp.int32, (1, pair_rows), 1)
        inside = n % rows
        place = (
            (n // rows) * (TILE_H * TILE_W)
            + (inside // FRAME_W % TILE_H) * TILE_W
            + inside % TILE_W
        )
        target = (slot_row.astype(jnp.int32) - pair * pair_tiles) * tile_len + place
        row = lax.broadcasted_iota(jnp.int32, (pair_rows, pair_rows), 0)
        perm[pair] = jnp.where(row == target, 1.0, 0.0).astype(jnp.bfloat16)

    is_dropped = drop_smem[0] == 1

    def null_sum(slot):
        landed(zall.at[slot, pl.ds(0, dp_count - 1)], z_recv.at[slot])
        total = zall[slot, 0].astype(jnp.float32)
        for peer in range(1, dp_count):
            total = total + zall[slot, peer].astype(jnp.float32)
        for t in range(2):
            nsum[slot, t] = total[t * prompt_rows : (t + 1) * prompt_rows].astype(jnp.bfloat16)
        cols = columns(head_of(me, slot))
        null_outward(slot, start)
        for t in range(2):
            pltpu.make_async_copy(
                nsum.at[slot, t], null_outs[t].at[:, cols], own_null.at[slot, t]
            ).start()

    def one_head(slot, carry):
        for t in range(4):
            landed(inbuf.at[slot, t], in_recv.at[slot, t])
        for t in range(2):
            landed(textbuf.at[slot, t], text_recv.at[slot, t])
            landed(nullbuf.at[slot, t], null_sem.at[slot, t])
        prompt = []
        for t in range(2):
            text = textbuf[slot, t].astype(jnp.float32).reshape(prompt_rows, HD)
            null = nullbuf[slot, t].astype(jnp.float32)
            prompt.append(jnp.where(is_dropped, null, text).astype(jnp.bfloat16))
        prompt_k, prompt_v = prompt
        prompt_dk = jnp.zeros((prompt_rows, HD), jnp.float32)
        prompt_dv = jnp.zeros((prompt_rows, HD), jnp.float32)
        acc_k[...] = jnp.zeros_like(acc_k)
        acc_v[...] = jnp.zeros_like(acc_v)
        for pair in range(chips):
            low, high = spans[pair]
            own = slice(pair * pair_rows, (pair + 1) * pair_rows)
            q = inbuf[slot, 0, own, :]
            go = inbuf[slot, 3, own, :]
            near_k = inbuf[slot, 1, low:high, :]
            near_v = inbuf[slot, 2, low:high, :]
            near = dot(near_k, q, NT) * score_scale + bias[pair, : high - low, :]
            text = dot(prompt_k, q, NT) * score_scale
            top = jnp.maximum(
                jnp.max(near, axis=0, keepdims=True), jnp.max(text, axis=0, keepdims=True)
            )
            near = jnp.exp(near - top)
            text = jnp.exp(text - top)
            share = 1.0 / (
                jnp.sum(near, axis=0, keepdims=True) + jnp.sum(text, axis=0, keepdims=True)
            )
            near = near * share
            text = text * share
            near_low = near.astype(jnp.bfloat16)
            text_low = text.astype(jnp.bfloat16)
            near_g = dot(near_v, go, NT)
            text_g = dot(prompt_v, go, NT)
            row_dot = jnp.sum(
                near_low.astype(jnp.float32) * near_g, axis=0, keepdims=True
            ) + jnp.sum(text_low.astype(jnp.float32) * text_g, axis=0, keepdims=True)
            near_ds = (near * (near_g - row_dot)).astype(jnp.bfloat16)
            text_ds = (text * (text_g - row_dot)).astype(jnp.bfloat16)
            dq = (dot(near_ds, near_k, TN) + dot(text_ds, prompt_k, TN)) * score_scale
            outbuf[slot, 0, own, :] = dot(perm[pair], dq.astype(jnp.bfloat16)).astype(jnp.bfloat16)
            acc_k[low:high, :] += dot(near_ds, q)
            acc_v[low:high, :] += dot(near_low, go)
            prompt_dk += dot(text_ds, q)
            prompt_dv += dot(text_low, go)
        prompt_dk = prompt_dk * score_scale
        drop_scale = jnp.where(is_dropped, 1.0, 0.0)
        keep_scale = 1.0 - drop_scale
        for t, grad in enumerate((prompt_dk, prompt_dv)):
            kept = (grad * keep_scale).reshape(seq_count, text_rows, HD)
            tgrad[slot, t] = kept.astype(jnp.bfloat16)
            zall[slot, clip, t * prompt_rows : (t + 1) * prompt_rows, :] = (
                grad * drop_scale
            ).astype(jnp.bfloat16)
        for off in range(1, dp_count):
            across_clips(slot, off).start()

        @pl.when(slot == 1)
        def _():
            null_sum(0)

        for off in range(1, seq_count):
            outward(slot, off, start, (0,))
        for pair in range(chips):
            own = slice(pair * pair_rows, (pair + 1) * pair_rows)
            dk = (acc_k[own, :] * score_scale).astype(jnp.bfloat16)
            outbuf[slot, 1, own, :] = dot(perm[pair], dk).astype(jnp.bfloat16)
            dv = acc_v[own, :].astype(jnp.bfloat16)
            outbuf[slot, 2, own, :] = dot(perm[pair], dv).astype(jnp.bfloat16)

        @pl.when(slot == 1)
        def _():
            null_sum(slot)

        for off in range(1, seq_count):
            outward(slot, off, start, (1, 2))
        outward_own(slot)
        return carry

    lax.fori_loop(0, own_slots, one_head, 0)

    @pl.when(parity == 1)
    def _():
        null_sum(0)


    def pass_on(slot, carry):
        for t in range(2):
            landed(null_outs[t].at[:, 0 : (chips - 1) * HD], n_recv.at[slot, t])
        null_relay(slot, start)
        return carry

    lax.fori_loop(0, own_slots, pass_on, 0)

    all_inward(sent)

    def drain(slot, carry):
        for off in range(1, dp_count):
            across_clips(slot, off).wait_send()
        for off in range(1, seq_count):
            outward(slot, off, sent)
        null_outward(slot, sent)
        null_relay(slot, sent)
        for t in range(2):
            landed(nsum.at[slot, t], own_null.at[slot, t])
        return carry

    def from_sibling(slot, carry):
        for t in range(2):
            for place in range(chips):
                landed(null_outs[t].at[:, 0:HD], sib_recv.at[slot, place, t])
        return carry

    lax.fori_loop(0, own_slots, drain, 0)
    for t in range(3):
        landed(outs[t], out_recv.at[t])
    for t in range(2):
        landed(text_outs[t], tg_recv.at[t])
    lax.fori_loop(0, 1 + parity, from_sibling, 0)


def hand_over(*refs):
    count = (len(refs) - 1) // 2
    sources, results, out_of = refs[:count], refs[count : 2 * count], refs[2 * count]
    stores = [pltpu.make_async_copy(sources[i], results[i], out_of.at[i]) for i in range(count)]
    for store in stores:
        store.start()
    for store in stores:
        store.wait()


def by_heads(
    dp_count,
    queries,
    keys,
    values,
    grad_out,
    text_keys,
    text_values,
    null_keys,
    null_values,
    windows,
    tile_slot,
    dropped,
):
    seq_count = lax.axis_size("seq")
    rows = queries.shape[1]
    total_rows = seq_count * rows
    pair_rows = 2 * rows
    text_rows = text_keys.shape[1]
    prompt_rows = text_rows * seq_count
    chips = seq_count // 2
    bf16, f32 = jnp.bfloat16, jnp.float32
    dma = pltpu.SemaphoreType.DMA
    hbm = pl.BlockSpec(memory_space=pl.ANY)
    like = [queries, keys, values, text_keys, text_values, null_keys, null_values]
    gathered = pl.pallas_call(
        functools.partial(head_kernel, seq_count, dp_count),
        out_shape=tuple(jax.ShapeDtypeStruct(x.shape, x.dtype) for x in like),
        in_specs=[hbm] * 11,
        out_specs=tuple([hbm] * 7),
        scratch_shapes=[
            pltpu.VMEM((SLOTS, 4, total_rows, HD), bf16),
            pltpu.VMEM((SLOTS, 2, seq_count, text_rows, HD), bf16),
            pltpu.VMEM((SLOTS, 2, prompt_rows, HD), bf16),
            pltpu.VMEM((SLOTS, 3, total_rows, HD), bf16),
            pltpu.VMEM((SLOTS, 2, seq_count, text_rows, HD), bf16),
            pltpu.VMEM((SLOTS, dp_count, 2 * prompt_rows, HD), bf16),
            pltpu.VMEM((SLOTS, 2, prompt_rows, HD), bf16),
            pltpu.VMEM((chips, 3 * pair_rows, pair_rows), f32),
            pltpu.VMEM((chips, pair_rows, pair_rows), bf16),
            pltpu.VMEM((total_rows, HD), f32),
            pltpu.VMEM((total_rows, HD), f32),
            dma((SLOTS, seq_count, 4)),
            dma((SLOTS, 4)),
            dma((SLOTS, seq_count, 2)),
            dma((SLOTS, 2)),
            dma((SLOTS, 2)),
            dma((SLOTS, seq_count, 3)),
            dma((3,)),
            dma((SLOTS, seq_count, 2)),
            dma((2,)),
            dma((SLOTS, dp_count)),
            dma((SLOTS,)),
            dma((SLOTS, chips, 2)),
            dma((SLOTS, 2)),
            dma((SLOTS, 2)),
            dma((SLOTS, chips, 2)),
            dma((SLOTS, chips, 2)),
            pltpu.VMEM(windows.shape[::-1], jnp.int32),
            pltpu.VMEM((1, tile_slot.shape[0]), jnp.int32),
            pltpu.SMEM(dropped.shape, jnp.int32),
            dma((3,)),
        ],
        compiler_params=pltpu.CompilerParams(
            collective_id=0, has_side_effects=True, vmem_limit_bytes=24 * 2**20
        ),
    )(
        *(
            pltpu.with_memory_space_constraint(x, pltpu.HBM)
            for x in (
                queries,
                keys,
                values,
                grad_out,
                text_keys,
                text_values,
                null_keys,
                null_values,
                windows.T,
                tile_slot.reshape(1, -1),
            )
        ),
        dropped,
    )
    return pl.pallas_call(
        hand_over,
        out_shape=tuple(jax.ShapeDtypeStruct(x.shape, x.dtype) for x in like),
        in_specs=[hbm] * 7,
        out_specs=tuple([hbm] * 7),
        scratch_shapes=[dma((7,))],
        compiler_params=pltpu.CompilerParams(vmem_limit_bytes=2 * 2**20),
    )(*gathered)


def device_program(mesh):
    seq_count, dp_count = mesh.shape["seq"], mesh.shape["dp"]

    def program(*arrays):
        head_count = arrays[0].shape[2] // HD
        if seq_count % 2 == 0 and 2 * head_count == HEADS_PER_PAIR * seq_count:
            return by_heads(dp_count, *arrays)
        return per_device(*arrays)

    return program


def solution(mesh):
    in_specs = (
        P("dp", "seq", None),
        P("dp", "seq", None),
        P("dp", "seq", None),
        P("dp", "seq", None),
        P("dp", "seq", None),
        P("dp", "seq", None),
        P(),
        P(),
        P(),
        P(),
        P("dp"),
    )
    out_specs = (
        P("dp", "seq", None),
        P("dp", "seq", None),
        P("dp", "seq", None),
        P("dp", "seq", None),
        P("dp", "seq", None),
        P(),
        P(),
    )
    return jax.shard_map(
        device_program(mesh), mesh=mesh, in_specs=in_specs, out_specs=out_specs, check_vma=False
    )
```
